256 devices in a mesh: dp: 4 (over x), seq: 8 (over z_lo, y), tensor: 8 (over z_hi, core).
Axes of the slice: x: 4, y: 4, z: 8 (z_hi: 4, z_lo: 2; z = z_hi * 2 + z_lo), core: 2. Of those that a mesh axis runs over, the one named last changes fastest.
Arguments:
- hidden: bfloat16 [4096, 28672], P(('dp', 'seq'), 'tensor'), may hold values from -6 to 6
- weight: bfloat16 [28672, 4096], P('tensor', 'seq'), may hold values from -0.03125 to 0.03125
- out_grad: bfloat16 [4096, 4096], P(('dp', 'tensor'), 'seq'), may hold values from -6 to 6
Outputs:
- output: bfloat16 [4096, 4096], P(('dp', 'tensor'), 'seq')
- grad_hidden: bfloat16 [4096, 28672], P(('dp', 'seq'), 'tensor')
- grad_weight: bfloat16 [28672, 4096], P('tensor', 'seq')
The draws below stay inside these ranges and needn't reach their ends.
All inputs are finite; a program needn't handle non-finite values.
Results may differ from the reference program's by a relative error of at most 0.017.
Values may be sent and summed in bfloat16 or wider, within the bound.
A program may use at most 128 MiB of HBM per device.

```python
import jax
import jax.numpy as jnp
from jax import lax

FF = 28672
DW = 4096
HB = 512
TOK_REP = 1024
TOKENS = 4096
SEQ_COLS = 512
N_TENSOR = 8


def block_scale(key, extent, cuts, least, high):
    factor_of = 1.0
    for dim, shards_of in cuts:
        steps = jax.random.uniform(jax.random.fold_in(jax.random.fold_in(key, 6), dim), (shards_of,), jnp.float32, least / len(cuts), high / len(cuts))
        factor_of = factor_of * jnp.repeat(jnp.exp(steps), extent[dim] // shards_of).reshape((-1,) + (1,) * (len(extent) - 1 - dim))
    return factor_of


def noise(rng, shape, deviation, most, pieces=(), kind=jnp.bfloat16):
    drawn = deviation * jax.random.normal(rng, shape, jnp.float32)
    if pieces:
        drawn = drawn * block_scale(rng, shape, pieces, -0.22, 0.18)
    return jnp.clip(drawn, -most, most).astype(kind)


def setup_inputs(seed: int = 0) -> dict:
    arg_keys = jax.random.split(jax.random.key(seed), 4)
    return {
        "hidden": noise(arg_keys[0], (TOKENS, FF), 1.0, 6.0, ((0, 32), (1, 8))),
        "weight": noise(arg_keys[1], (FF, DW), FF ** -0.5, 0.03125, ((0, 8), (1, 8))),
        "out_grad": noise(arg_keys[2], (TOKENS, DW), 1.0, 6.0, ((0, 32), (1, 8))),
    }


def sylvester(table_order):
    matrix = jnp.ones((1, 1), jnp.float32)
    while matrix.shape[0] < table_order:
        matrix = jnp.concatenate([jnp.concatenate([matrix, matrix], 1), jnp.concatenate([matrix, -matrix], 1)], 0)
    return matrix


def rounded(values):
    return lax.optimization_barrier(values.astype(jnp.bfloat16)).astype(jnp.float32)


def rotate(values):
    row_count = values.shape[0]
    shaped = values.astype(jnp.float32).reshape(row_count, N_TENSOR, FF // (N_TENSOR * HB), HB)
    mixed_rows = jnp.einsum("rtbk,kl->rtbl", shaped, sylvester(HB), precision=lax.Precision.HIGHEST)
    mixed_rows = jnp.einsum("rtbl,ts->rsbl", mixed_rows, sylvester(N_TENSOR), precision=lax.Precision.HIGHEST)
    return mixed_rows.reshape(row_count, FF) * (1.0 / float(N_TENSOR * HB) ** 0.5)


def reference(hidden, weight, out_grad):
    rotated = rotate(hidden).astype(jnp.bfloat16)
    output = jnp.dot(rotated, weight, preferred_element_type=jnp.float32).astype(jnp.bfloat16)
    grad_scale = 1.0 / float(TOKENS) ** 0.5
    grad_sum = jnp.zeros((FF, DW), jnp.float32)
    for replica in range(TOKENS // TOK_REP):
        rows_now = rotated[replica * TOK_REP:(replica + 1) * TOK_REP]
        grads_now = out_grad[replica * TOK_REP:(replica + 1) * TOK_REP]
        grad_sum = grad_sum + rounded(jnp.dot(rows_now.T, grads_now, preferred_element_type=jnp.float32) * grad_scale)
    grad_weight = grad_sum.astype(jnp.bfloat16)
    rotated_grad = jnp.zeros((TOKENS, FF), jnp.float32)
    for block_index in range(DW // SEQ_COLS):
        grad_block = out_grad[:, block_index * SEQ_COLS:(block_index + 1) * SEQ_COLS]
        weight_block = weight[:, block_index * SEQ_COLS:(block_index + 1) * SEQ_COLS]
        rotated_grad = rotated_grad + rounded(jnp.dot(grad_block, weight_block.T, preferred_element_type=jnp.float32))
    grad_hidden = rotate(rotated_grad).astype(jnp.bfloat16)
    return output, grad_hidden, grad_weight
```

```python
import jax
import jax.numpy as jnp
from jax import lax
from jax.experimental import pallas as pl
from jax.experimental.pallas import tpu as pltpu
from jax.sharding import PartitionSpec as P

HB = 512
NB = 7
BF = jnp.bfloat16
F32 = jnp.float32
MESH = pl.DeviceIdType.MESH
STAGES = ("f1", "g", "f2", "f3l", "f3r", "f4", "x1", "x2", "b1l", "b1r", "b2", "b3", "b4", "o")


def parity_table():
    row = lax.broadcasted_iota(jnp.int32, (HB, HB), 0)
    col = lax.broadcasted_iota(jnp.int32, (HB, HB), 1)
    both = row & col
    both = both ^ (both >> 8)
    both = both ^ (both >> 4)
    both = both ^ (both >> 2)
    both = both ^ (both >> 1)
    return jnp.where((both & 1) == 1, -1.0, 1.0).astype(BF)


def walsh8(parts):
    for bit in (1, 2, 4):
        parts = [
            parts[i] + parts[i ^ bit] if i & bit == 0 else parts[i ^ bit] - parts[i]
            for i in range(8)
        ]
    return parts


def kernel(hid, wgt, ogr, out, ghid, gwgt, a, r, hg, p, q1, q2, s, z, t2, d, xr, dd, gv, wv, oa, op, orx, tab, recv, send, wsem):
    x = lax.axis_index("dp")
    sq = lax.axis_index("seq")
    tn = lax.axis_index("tensor")
    zl = sq // 4
    y = sq % 4
    yr = (y + 1) % 4
    yl = (y + 3) % 4
    yo = (y + 2) % 4
    right = (x, zl * 4 + yr, tn)
    left = (x, zl * 4 + yl, tn)

    def R(name, j):
        return recv.at[STAGES.index(name), j]

    def S(name, j):
        return send.at[STAGES.index(name), j]

    def rows(n):
        return wv.at[pl.ds(0, n)]

    def wait(sem, n):
        pltpu.make_async_copy(rows(n), rows(n), sem).wait()

    def put(src, dst, name, j, dev, sname=None):
        pltpu.make_async_remote_copy(
            src_ref=src, dst_ref=dst, send_sem=S(sname or name, j), recv_sem=R(name, j),
            device_id=dev, device_id_type=MESH,
        ).start()

    def local(src, dst, name, j):
        pltpu.make_async_copy(src, dst, R(name, j)).start()

    def cols(j):
        return pl.ds(pl.multiple_of(j * HB, HB), HB)

    def r16(i):
        return pl.ds(pl.multiple_of(i * 16, 16), 16)

    wcopy = pltpu.make_async_copy(wgt, wv, wsem)
    wcopy.start()

    bar = pltpu.get_barrier_semaphore()
    peers = [(x, sq, (tn + k) % 8) for k in range(1, 8)]
    peers += [(x, (sq + 4) % 8, (tn + k) % 8) for k in range(8)]
    peers += [right, left]
    peers += [((x + k) % 4, sq, tn) for k in range(1, 4)]
    for dev in peers:
        pl.semaphore_signal(bar, inc=1, device_id=dev, device_id_type=MESH)
    pl.semaphore_wait(bar, len(peers))

    def f1(j):
        for k in range(1, 8):
            to = (tn + k) % 8
            put(hid.at[r16(to), cols(j)], a.at[j, tn], "f1", j, (x, sq, to))
        local(hid.at[r16(tn), cols(j)], a.at[j, tn], "f1", j)

    f1(0)
    for k in range(1, 8):
        put(ogr, gv.at[tn], "g", 0, (x, sq, (tn + k) % 8))
    local(ogr, gv.at[tn], "g", 0)

    @pl.loop(1, NB)
    def _(j):
        f1(j)

    tab[...] = parity_table()
    oa[...] = jnp.zeros_like(oa)

    def rotate_to(mixed, dst, j):
        parts = walsh8([mixed[i * 16:(i + 1) * 16] for i in range(8)])
        for i in range(8):
            dst[j, i] = (parts[i] * (1.0 / 64.0)).astype(BF)

    def spread(src, dst, name, j):
        for zk in range(2):
            zt = (zl + zk) % 2
            for k in range(8):
                to = (tn + k) % 8
                if zk == 0 and k == 0:
                    local(src(zl, tn), dst, name, j)
                else:
                    put(src(zt, to), dst, name, j, (x, zt * 4 + y, to))

    def f2(j):
        wait(R("f1", j), 128)
        mixed = jnp.dot(a[j].reshape(128, HB), tab[...], preferred_element_type=F32)
        rotate_to(mixed, r, j)
        spread(lambda zt, to: r.at[j, to], hg.at[j, zl, y, tn], "f2", j)

    def f3(j):
        wait(R("f2", j), 256)
        put(hg.at[j, :, y], hg.at[j, :, y], "f3l", j, right)
        put(hg.at[j, :, y], hg.at[j, :, y], "f3r", j, left)

    def f4(j):
        wait(R("f3l", j), 256)
        put(hg.at[j, 0, yl], hg.at[j, 0, yl], "f4", j, right)
        wait(R("f3r", j), 256)
        put(hg.at[j, 1, yr], hg.at[j, 1, yr], "f4", j, left)

    def wj(j):
        return wv[pl.ds(pl.multiple_of(j * HB, HB), HB), :]

    def f5(j):
        wait(R("f4", j), 256)
        whole = hg[j].reshape(1024, HB)
        grad = lax.dot_general(
            whole, gv[...].reshape(1024, HB), (((0,), (0,)), ((), ())), preferred_element_type=F32
        )
        d[j] = (grad * (1.0 / 64.0)).astype(BF).reshape(4, 128, HB)
        for k in range(1, 4):
            to = (x + k) % 4
            put(d.at[j, to], xr.at[j, k - 1], "x1", j, (to, sq, tn))
        oa[...] += jnp.dot(whole, wj(j), preferred_element_type=F32)

    def x2(j):
        wait(R("x1", j), 384)
        total = d[j, x].astype(F32)
        for k in range(3):
            total = total + xr[j, k].astype(F32)
        dd[j] = total.astype(BF)
        mine = gwgt.at[pl.ds(pl.multiple_of(j * HB + x * 128, 128), 128)]
        for k in range(1, 4):
            put(dd.at[j], mine, "x2", j, ((x + k) % 4, sq, tn))
        local(dd.at[j], mine, "x2", j)

    def b1(j):
        part = lax.dot_general(
            gv[...].reshape(1024, HB), wj(j), (((1,), (1,)), ((), ())), preferred_element_type=F32
        )
        p[j] = part.astype(BF).reshape(2, 4, 128, HB)
        put(p.at[j, 0, yo], q1.at[j, 0], "b1l", j, right)
        put(p.at[j, 1, yo], q1.at[j, 1], "b1r", j, left)

    def b2(j):
        wait(R("b1l", j), 128)
        p[j, 0, yr] = (p[j, 0, yr].astype(F32) + q1[j, 0].astype(F32)).astype(BF)
        put(p.at[j, :, yr], q2.at[j, 0], "b2", j, right)
        wait(R("b1r", j), 128)
        p[j, 1, yl] = (p[j, 1, yl].astype(F32) + q1[j, 1].astype(F32)).astype(BF)
        put(p.at[j, :, yl], q2.at[j, 1], "b2", j, left)

    def b3(j):
        wait(R("b2", j), 512)
        total = p[j, :, y].astype(F32) + q2[j, 0].astype(F32) + q2[j, 1].astype(F32)
        s[j] = total.astype(BF).reshape(2, 8, 16, HB)
        spread(lambda zt, to: s.at[j, zt, to], z.at[j, zl, tn], "b3", j)

    def b4(j):
        wait(R("b3", j), 256)
        mixed = jnp.dot(z[j, 0].reshape(128, HB), tab[...], preferred_element_type=F32)
        mixed = mixed + jnp.dot(z[j, 1].reshape(128, HB), tab[...], preferred_element_type=F32)
        rotate_to(mixed, t2, j)
        mine = ghid.at[r16(tn), cols(j)]
        for k in range(1, 8):
            to = (tn + k) % 8
            put(t2.at[j, to], mine, "b4", j, (x, sq, to))
        local(t2.at[j, tn], mine, "b4", j)

    f2(0)
    wcopy.wait()
    wait(R("g", 0), 1024)

    @pl.loop(0, NB + 1)
    def _(j):
        @pl.when(j < NB)
        def _():
            f3(j)
            b1(j)

        @pl.when(j == NB)
        def _():
            op[...] = oa[...].astype(BF).reshape(8, 128, HB)
            for k in range(1, 8):
                to = (tn + k) % 8
                put(op.at[to], orx.at[k - 1], "o", 0, (x, sq, to))

        @pl.when(j >= 1)
        def _():
            b3(j - 1)

        @pl.when(j + 1 < NB)
        def _():
            f2(j + 1)

        @pl.when(j < NB)
        def _():
            f4(j)
            b2(j)

        @pl.when(j >= 1)
        def _():
            x2(j - 1)
            b4(j - 1)

        @pl.when(j < NB)
        def _():
            f5(j)

    wait(R("o", 0), 896)
    total = op[tn].astype(F32)
    for k in range(7):
        total = total + orx[k].astype(F32)
    out[...] = total.astype(BF)

    wait(S("g", 0), 896)
    wait(S("o", 0), 896)

    @pl.loop(0, NB)
    def _(j):
        wait(R("x2", j), 512)
        wait(R("b4", j), 128)
        for name, n in (("f1", 112), ("f2", 240), ("f3l", 256), ("f3r", 256), ("f4", 256), ("x1", 384),
                        ("x2", 384), ("b1l", 128), ("b1r", 128), ("b2", 512), ("b3", 240), ("b4", 112)):
            wait(S(name, j), n)


def body(hidden, weight, out_grad):
    vm = pltpu.VMEM
    ns = len(STAGES)
    return pl.pallas_call(
        kernel,
        name="rotated_projection",
        out_shape=(
            jax.ShapeDtypeStruct((128, HB), BF),
            jax.ShapeDtypeStruct((128, NB * HB), BF),
            jax.ShapeDtypeStruct((NB * HB, HB), BF),
        ),
        in_specs=[pl.BlockSpec(memory_space=pl.ANY)] * 3,
        out_specs=(
            pl.BlockSpec(memory_space=pltpu.VMEM),
            pl.BlockSpec(memory_space=pl.ANY),
            pl.BlockSpec(memory_space=pl.ANY),
        ),
        scratch_shapes=[
            vm((NB, 8, 16, HB), BF),
            vm((NB, 8, 16, HB), BF),
            vm((NB, 2, 4, 8, 16, HB), BF),
            vm((NB, 2, 4, 128, HB), BF),
            vm((NB, 2, 128, HB), BF),
            vm((NB, 2, 2, 128, HB), BF),
            vm((NB, 2, 8, 16, HB), BF),
            vm((NB, 2, 8, 16, HB), BF),
            vm((NB, 8, 16, HB), BF),
            vm((NB, 4, 128, HB), BF),
            vm((NB, 3, 128, HB), BF),
            vm((NB, 128, HB), BF),
            vm((8, 128, HB), BF),
            vm((NB * HB, HB), BF),
            vm((1024, HB), F32),
            vm((8, 128, HB), BF),
            vm((7, 128, HB), BF),
            vm((HB, HB), BF),
            pltpu.SemaphoreType.DMA((ns, NB)),
            pltpu.SemaphoreType.DMA((ns, NB)),
            pltpu.SemaphoreType.DMA,
        ],
        compiler_params=pltpu.CompilerParams(
            collective_id=0, has_side_effects=True, vmem_limit_bytes=60 * 1024 * 1024
        ),
    )(hidden, weight, out_grad)


def solution(mesh):
    in_specs = (P(("dp", "seq"), "tensor"), P("tensor", "seq"), P(("dp", "tensor"), "seq"))
    out_specs = (P(("dp", "tensor"), "seq"), P(("dp", "seq"), "tensor"), P("tensor", "seq"))
    return jax.shard_map(body, mesh=mesh, in_specs=in_specs, out_specs=out_specs, check_vma=False)
```

```python
import jax
import jax.numpy as jnp
from jax import lax
from jax.experimental import pallas as pl
from jax.experimental.pallas import tpu as pltpu
from jax.sharding import PartitionSpec as P

HB = 512
NB = 7
BF = jnp.bfloat16
F32 = jnp.float32
MESH = pl.DeviceIdType.MESH
STAGES = (
    "f1", "g1", "g2", "f2", "f2b", "f3l", "f3r", "f4", "x1", "x2",
    "b1l", "b1r", "b2", "b3a", "b3", "b4", "o1", "o2",
)


def parity_table():
    row = lax.broadcasted_iota(jnp.int32, (HB, HB), 0)
    col = lax.broadcasted_iota(jnp.int32, (HB, HB), 1)
    both = row & col
    both = both ^ (both >> 8)
    both = both ^ (both >> 4)
    both = both ^ (both >> 2)
    both = both ^ (both >> 1)
    return jnp.where((both & 1) == 1, -1.0, 1.0).astype(BF)


def walsh8(parts):
    for bit in (1, 2, 4):
        parts = [
            parts[i] + parts[i ^ bit] if i & bit == 0 else parts[i ^ bit] - parts[i]
            for i in range(8)
        ]
    return parts


def kernel(hid, wgt, ogr, out, ghid, gwgt, a, r, hg, p, q1, q2, s, zz, s2, z, t2, d, xr, dd, gv, wv, oa, op, oh, o2, orx, tab, recv, send, wsem):
    x = lax.axis_index("dp")
    sq = lax.axis_index("seq")
    tn = lax.axis_index("tensor")
    zl = sq // 4
    y = sq % 4
    yr = (y + 1) % 4
    yl = (y + 3) % 4
    yo = (y + 2) % 4
    right = (x, zl * 4 + yr, tn)
    left = (x, zl * 4 + yl, tn)
    zh = tn // 2
    co = tn % 2
    beside = (x, (1 - zl) * 4 + y, tn)
    twin = (x, sq, zh * 2 + 1 - co)

    def near_sites(lo):
        e = (zh + 3 + 2 * lo) % 4
        return ((0, e), (1, e), (1 - lo, (zh + 2) % 4), (lo, zh))

    def near_lo(k):
        return (zl, 0, 1 - zl, 1)[k]

    def R(name, j):
        return recv.at[STAGES.index(name), j]

    def S(name, j):
        return send.at[STAGES.index(name), j]

    def rows(n):
        return wv.at[pl.ds(0, n)]

    def wait(sem, n):
        pltpu.make_async_copy(rows(n), rows(n), sem).wait()

    def put(src, dst, name, j, dev, sname=None):
        pltpu.make_async_remote_copy(
            src_ref=src, dst_ref=dst, send_sem=S(sname or name, j), recv_sem=R(name, j),
            device_id=dev, device_id_type=MESH,
        ).start()

    def local(src, dst, name, j):
        pltpu.make_async_copy(src, dst, R(name, j)).start()

    def cols(j):
        return pl.ds(pl.multiple_of(j * HB, HB), HB)

    def r16(i):
        return pl.ds(pl.multiple_of(i * 16, 16), 16)

    wcopy = pltpu.make_async_copy(wgt, wv, wsem)
    wcopy.start()

    bar = pltpu.get_barrier_semaphore()
    peers = [(x, sq, (tn + k) % 8) for k in range(1, 8)]
    peers += [(x, (sq + 4) % 8, (tn + k) % 8) for k in range(8)]
    peers += [right, left]
    peers += [((x + k) % 4, sq, tn) for k in range(1, 4)]
    for dev in peers:
        pl.semaphore_signal(bar, inc=1, device_id=dev, device_id_type=MESH)
    pl.semaphore_wait(bar, len(peers))

    def f1(j):
        for k in range(1, 8):
            to = (tn + k) % 8
            put(hid.at[r16(to), cols(j)], a.at[j, tn], "f1", j, (x, sq, to))
        local(hid.at[r16(tn), cols(j)], a.at[j, tn], "f1", j)

    def g1(k):
        put(ogr, gv.at[tn], "g1", 0, (x, sq, (tn + 2 * k) % 8))

    def g0():
        put(ogr, gv.at[tn], "g2", 0, twin)
        local(ogr, gv.at[tn], "g1", 0)

    def g2():
        wait(R("g1", 0), 512)
        for k in range(1, 4):
            part = (tn + 2 * k) % 8
            put(gv.at[part], gv.at[part], "g2", 0, twin)

    f1(0)
    g0()
    for k in (1, 3, 2):
        g1(k)
    tab[...] = parity_table()
    oa[...] = jnp.zeros_like(oa)

    def rotate_to(mixed, dst, j):
        parts = walsh8([mixed[i * 16:(i + 1) * 16] for i in range(8)])
        for i in range(8):
            dst[j, i] = (parts[i] * (1.0 / 64.0)).astype(BF)

    def f2(j):
        wait(R("f1", j), 128)
        mixed = jnp.dot(a[j].reshape(128, HB), tab[...], preferred_element_type=F32)
        rotate_to(mixed, r, j)
        land = hg.at[j, zl, y, tn]
        for k in range(4):
            for c in range(2):
                to = ((zh + k) % 4) * 2 + (co + c) % 2
                if k == 0 and c == 0:
                    local(r.at[j, tn], land, "f2", j)
                else:
                    put(r.at[j, to], land, "f2", j, (x, near_lo(k) * 4 + y, to))

    def f2b(j):
        wait(R("f2", j), 128)
        for lo, hi in near_sites(zl):
            part = hg.at[j, lo, y, pl.ds(hi * 2, 2)]
            put(part, part, "f2b", j, beside)

    def f3(j):
        wait(R("f2b", j), 128)
        put(hg.at[j, :, y], hg.at[j, :, y], "f3l", j, right)
        put(hg.at[j, :, y], hg.at[j, :, y], "f3r", j, left)

    def f4(j):
        wait(R("f3l", j), 256)
        put(hg.at[j, 0, yl], hg.at[j, 0, yl], "f4", j, right)
        wait(R("f3r", j), 256)
        put(hg.at[j, 1, yr], hg.at[j, 1, yr], "f4", j, left)

    def wj(j):
        return wv[pl.ds(pl.multiple_of(j * HB, HB), HB), :]

    def f5a(j):
        wait(R("f4", j), 256)
        oa[...] += jnp.dot(hg[j].reshape(1024, HB), wj(j), preferred_element_type=F32)

    def f5b(j):
        grad = lax.dot_general(
            hg[j].reshape(1024, HB), gv[...].reshape(1024, HB), (((0,), (0,)), ((), ())),
            preferred_element_type=F32,
        )
        d[j] = (grad * (1.0 / 64.0)).astype(BF).reshape(4, 128, HB)
        for k in range(1, 4):
            to = (x + k) % 4
            put(d.at[j, to], xr.at[j, k - 1], "x1", j, (to, sq, tn))

    def x2(j):
        wait(R("x1", j), 384)
        total = d[j, x].astype(F32)
        for k in range(3):
            total = total + xr[j, k].astype(F32)
        dd[j] = total.astype(BF)
        mine = gwgt.at[pl.ds(pl.multiple_of(j * HB + x * 128, 128), 128)]
        for k in range(1, 4):
            put(dd.at[j], mine, "x2", j, ((x + k) % 4, sq, tn))
        local(dd.at[j], mine, "x2", j)

    def b1(j):
        part = lax.dot_general(
            gv[...].reshape(1024, HB), wj(j), (((1,), (1,)), ((), ())), preferred_element_type=F32
        )
        p[j] = part.astype(BF).reshape(2, 4, 128, HB)
        put(p.at[j, 0, yo], q1.at[j, 0], "b1l", j, right)
        put(p.at[j, 1, yo], q1.at[j, 1], "b1r", j, left)

    def b2(j):
        wait(R("b1l", j), 128)
        p[j, 0, yr] = (p[j, 0, yr].astype(F32) + q1[j, 0].astype(F32)).astype(BF)
        put(p.at[j, :, yr], q2.at[j, 0], "b2", j, right)
        wait(R("b1r", j), 128)
        p[j, 1, yl] = (p[j, 1, yl].astype(F32) + q1[j, 1].astype(F32)).astype(BF)
        put(p.at[j, :, yl], q2.at[j, 1], "b2", j, left)

    def b3a(j):
        wait(R("b2", j), 512)
        total = p[j, :, y].astype(F32) + q2[j, 0].astype(F32) + q2[j, 1].astype(F32)
        s[j] = total.astype(BF).reshape(2, 8, 16, HB)
        for i, (lo, hi) in enumerate(near_sites(1 - zl)):
            put(s.at[j, lo, pl.ds(hi * 2, 2)], zz.at[j, i], "b3a", j, beside)

    def b3(j):
        wait(R("b3a", j), 128)
        for i, (lo, hi) in enumerate(near_sites(zl)):
            pair = s[j, lo, pl.ds(hi * 2, 2)].astype(F32) + zz[j, i].astype(F32)
            s2[j, i] = pair.astype(BF)
        for i, (lo, hi) in enumerate(near_sites(zl)):
            for c in range(2):
                cc = (co + c) % 2
                if i == 3 and c == 0:
                    local(s2.at[j, i, cc], z.at[j, tn], "b3", j)
                else:
                    put(s2.at[j, i, cc], z.at[j, tn], "b3", j, (x, lo * 4 + y, hi * 2 + cc))

    def b4(j):
        wait(R("b3", j), 128)
        mixed = jnp.dot(z[j].reshape(128, HB), tab[...], preferred_element_type=F32)
        rotate_to(mixed, t2, j)
        mine = ghid.at[r16(tn), cols(j)]
        for k in range(1, 8):
            to = (tn + k) % 8
            put(t2.at[j, to], mine, "b4", j, (x, sq, to))
        local(t2.at[j, tn], mine, "b4", j)

    def o1():
        op[...] = oa[...].astype(BF).reshape(4, 2, 128, HB)
        for k in range(4):
            put(op.at[k, 1 - co], oh.at[k], "o1", 0, twin)

    def o2s():
        wait(R("o1", 0), 512)
        for k in range(4):
            o2[k] = (op[k, co].astype(F32) + oh[k].astype(F32)).astype(BF)
        for k in range(1, 4):
            to = (zh + k) % 4
            put(o2.at[to], orx.at[k - 1], "o2", 0, (x, sq, to * 2 + co))

    def at(cond, *steps):
        @pl.when(cond)
        def _():
            for step in steps:
                step()

    f2(0)
    f1(1)
    g2()
    wcopy.wait()
    wait(R("g2", 0), 512)
    b1(0)
    f2b(0)
    f2(1)
    f1(2)
    f3(0)

    @pl.loop(0, NB)
    def _(j):
        prev = j >= 1
        more = j + 1 < NB
        b2(j)
        at(j + 3 < NB, lambda: f1(j + 3))
        at(prev, lambda: b3a(j - 1))
        at(j + 2 < NB, lambda: f2(j + 2))
        f4(j)
        at(prev, lambda: b3(j - 1))
        at(more, lambda: b1(j + 1), lambda: f2b(j + 1), lambda: f3(j + 1))
        at(prev, lambda: x2(j - 1))
        at(j + 1 == NB, lambda: b3a(j))
        f5a(j)
        at(j + 1 == NB, o1)
        f5b(j)
        at(prev, lambda: b4(j - 1))

    b3(NB - 1)
    o2s()
    x2(NB - 1)
    b4(NB - 1)

    wait(R("o2", 0), 384)
    total = o2[zh].astype(F32)
    for k in range(3):
        total = total + orx[k].astype(F32)
    out[...] = total.astype(BF)

    for name, n in (("g1", 384), ("g2", 512), ("o1", 512), ("o2", 384)):
        wait(S(name, 0), n)

    @pl.loop(0, NB)
    def _(j):
        wait(R("x2", j), 512)
        wait(R("b4", j), 128)
        for name, n in (("f1", 112), ("f2", 112), ("f2b", 128), ("f3l", 256), ("f3r", 256), ("f4", 256), ("x1", 384),
                        ("x2", 384), ("b1l", 128), ("b1r", 128), ("b2", 512), ("b3a", 128), ("b3", 112), ("b4", 112)):
            wait(S(name, j), n)


def body(hidden, weight, out_grad):
    vm = pltpu.VMEM
    ns = len(STAGES)
    return pl.pallas_call(
        kernel,
        name="rotated_projection",
        out_shape=(
            pltpu.VMEM((128, HB), BF),
            pltpu.VMEM((128, NB * HB), BF),
            pltpu.VMEM((NB * HB, HB), BF),
        ),
        in_specs=[pl.BlockSpec(memory_space=pl.ANY)] * 3,
        out_specs=(pl.BlockSpec(memory_space=pltpu.VMEM),) * 3,
        scratch_shapes=[
            vm((NB, 8, 16, HB), BF),
            vm((NB, 8, 16, HB), BF),
            vm((NB, 2, 4, 8, 16, HB), BF),
            vm((NB, 2, 4, 128, HB), BF),
            vm((NB, 2, 128, HB), BF),
            vm((NB, 2, 2, 128, HB), BF),
            vm((NB, 2, 8, 16, HB), BF),
            vm((NB, 4, 2, 16, HB), BF),
            vm((NB, 4, 2, 16, HB), BF),
            vm((NB, 8, 16, HB), BF),
            vm((NB, 8, 16, HB), BF),
            vm((NB, 4, 128, HB), BF),
            vm((NB, 3, 128, HB), BF),
            vm((NB, 128, HB), BF),
            vm((8, 128, HB), BF),
            vm((NB * HB, HB), BF),
            vm((1024, HB), F32),
            vm((4, 2, 128, HB), BF),
            vm((4, 128, HB), BF),
            vm((4, 128, HB), BF),
            vm((3, 128, HB), BF),
            vm((HB, HB), BF),
            pltpu.SemaphoreType.DMA((ns, NB)),
            pltpu.SemaphoreType.DMA((ns, NB)),
            pltpu.SemaphoreType.DMA,
        ],
        compiler_params=pltpu.CompilerParams(
            collective_id=0, has_side_effects=True, vmem_limit_bytes=54 * 1024 * 1024
        ),
    )(hidden, weight, out_grad)


def solution(mesh):
    in_specs = (P(("dp", "seq"), "tensor"), P("tensor", "seq"), P(("dp", "tensor"), "seq"))
    out_specs = (P(("dp", "tensor"), "seq"), P(("dp", "seq"), "tensor"), P("tensor", "seq"))
    return jax.shard_map(body, mesh=mesh, in_specs=in_specs, out_specs=out_specs, check_vma=False)
```

```python
import jax
import jax.numpy as jnp
from jax import lax
from jax.experimental import pallas as pl
from jax.experimental.pallas import tpu as pltpu
from jax.sharding import PartitionSpec as P

HB = 512
NB = 7
BF = jnp.bfloat16
F32 = jnp.float32
MESH = pl.DeviceIdType.MESH
STAGES = (
    "f1", "g1", "g2", "f2", "f2b", "f3l", "f3r", "f4", "x1", "x2",
    "b1l", "b1r", "b2", "b3a", "b3", "b4", "o1", "o2",
)


def parity_table():
    row = lax.broadcasted_iota(jnp.int32, (HB, HB), 0)
    col = lax.broadcasted_iota(jnp.int32, (HB, HB), 1)
    both = row & col
    both = both ^ (both >> 8)
    both = both ^ (both >> 4)
    both = both ^ (both >> 2)
    both = both ^ (both >> 1)
    return jnp.where((both & 1) == 1, -1.0, 1.0).astype(BF)


def walsh8(parts):
    for bit in (1, 2, 4):
        parts = [
            parts[i] + parts[i ^ bit] if i & bit == 0 else parts[i ^ bit] - parts[i]
            for i in range(8)
        ]
    return parts


def kernel(hid, wgt, ogr, out, ghid, gwgt, a, r, hg, p, q1, q2, s, zz, s2, z, t2, d, xr, dd, gv, wv, oa, op, oh, o2, orx, tab, recv, send, wsem):
    x = lax.axis_index("dp")
    sq = lax.axis_index("seq")
    tn = lax.axis_index("tensor")
    zl = sq // 4
    y = sq % 4
    yr = (y + 1) % 4
    yl = (y + 3) % 4
    yo = (y + 2) % 4
    right = (x, zl * 4 + yr, tn)
    left = (x, zl * 4 + yl, tn)
    zh = tn // 2
    co = tn % 2
    beside = (x, (1 - zl) * 4 + y, tn)
    twin = (x, sq, zh * 2 + 1 - co)

    def near_sites(lo):
        e = (zh + 3 + 2 * lo) % 4
        return ((0, e), (1, e), (1 - lo, (zh + 2) % 4), (lo, zh))

    def near_lo(k):
        return (zl, 0, 1 - zl, 1)[k]

    def R(name, j):
        return recv.at[STAGES.index(name), j]

    def S(name, j):
        return send.at[STAGES.index(name), j]

    def rows(n):
        return wv.at[pl.ds(0, n)]

    def wait(sem, n):
        pltpu.make_async_copy(rows(n), rows(n), sem).wait()

    def put(src, dst, name, j, dev, sname=None):
        pltpu.make_async_remote_copy(
            src_ref=src, dst_ref=dst, send_sem=S(sname or name, j), recv_sem=R(name, j),
            device_id=dev, device_id_type=MESH,
        ).start()

    def local(src, dst, name, j):
        pltpu.make_async_copy(src, dst, R(name, j)).start()

    def cols(j):
        return pl.ds(pl.multiple_of(j * HB, HB), HB)

    def r16(i):
        return pl.ds(pl.multiple_of(i * 16, 16), 16)

    wcopy = pltpu.make_async_copy(wgt, wv, wsem)
    wcopy.start()

    bar = pltpu.get_barrier_semaphore()
    peers = [(x, sq, (tn + k) % 8) for k in range(1, 8)]
    peers += [(x, (sq + 4) % 8, (tn + k) % 8) for k in range(8)]
    peers += [right, left]
    peers += [((x + k) % 4, sq, tn) for k in range(1, 4)]
    for dev in peers:
        pl.semaphore_signal(bar, inc=1, device_id=dev, device_id_type=MESH)
    pl.semaphore_wait(bar, len(peers))

    def f1(j):
        for k in range(1, 8):
            to = (tn + k) % 8
            put(hid.at[r16(to), cols(j)], a.at[j, tn], "f1", j, (x, sq, to))
        local(hid.at[r16(tn), cols(j)], a.at[j, tn], "f1", j)

    def g1(k):
        put(ogr, gv.at[tn], "g1", 0, (x, sq, (tn + 2 * k) % 8))

    def g0():
        put(ogr, gv.at[tn], "g2", 0, twin)
        local(ogr, gv.at[tn], "g1", 0)

    def g2():
        wait(R("g1", 0), 512)
        for k in range(1, 4):
            part = (tn + 2 * k) % 8
            put(gv.at[part], gv.at[part], "g2", 0, twin)

    g0()
    for k in (1, 3, 2):
        g1(k)
    f1(0)
    tab[...] = parity_table()
    oa[...] = jnp.zeros_like(oa)

    def rotate_to(mixed, dst, j):
        parts = walsh8([mixed[i * 16:(i + 1) * 16] for i in range(8)])
        for i in range(8):
            dst[j, i] = (parts[i] * (1.0 / 64.0)).astype(BF)

    def f2(j):
        wait(R("f1", j), 128)
        mixed = jnp.dot(a[j].reshape(128, HB), tab[...], preferred_element_type=F32)
        rotate_to(mixed, r, j)
        land = hg.at[j, zl, y, tn]
        for k in range(4):
            for c in range(2):
                to = ((zh + k) % 4) * 2 + (co + c) % 2
                if k == 0 and c == 0:
                    local(r.at[j, tn], land, "f2", j)
                else:
                    put(r.at[j, to], land, "f2", j, (x, near_lo(k) * 4 + y, to))

    def f2b(j):
        wait(R("f2", j), 128)
        for lo, hi in near_sites(zl):
            part = hg.at[j, lo, y, pl.ds(hi * 2, 2)]
            put(part, part, "f2b", j, beside)

    def f3(j):
        wait(R("f2b", j), 128)
        put(hg.at[j, :, y], hg.at[j, :, y], "f3l", j, right)
        put(hg.at[j, :, y], hg.at[j, :, y], "f3r", j, left)

    def f4(j):
        wait(R("f3l", j), 256)
        put(hg.at[j, 0, yl], hg.at[j, 0, yl], "f4", j, right)
        wait(R("f3r", j), 256)
        put(hg.at[j, 1, yr], hg.at[j, 1, yr], "f4", j, left)

    def wj(j):
        return wv[pl.ds(pl.multiple_of(j * HB, HB), HB), :]

    def f5a(j):
        wait(R("f4", j), 256)
        oa[...] += jnp.dot(hg[j].reshape(1024, HB), wj(j), preferred_element_type=F32)

    def f5b(j):
        grad = lax.dot_general(
            hg[j].reshape(1024, HB), gv[...].reshape(1024, HB), (((0,), (0,)), ((), ())),
            preferred_element_type=F32,
        )
        d[j] = (grad * (1.0 / 64.0)).astype(BF).reshape(4, 128, HB)
        for k in range(1, 4):
            to = (x + k) % 4
            put(d.at[j, to], xr.at[j, k - 1], "x1", j, (to, sq, tn))

    def x2(j):
        wait(R("x1", j), 384)
        total = d[j, x].astype(F32)
        for k in range(3):
            total = total + xr[j, k].astype(F32)
        dd[j] = total.astype(BF)
        mine = gwgt.at[pl.ds(pl.multiple_of(j * HB + x * 128, 128), 128)]
        for k in range(1, 4):
            put(dd.at[j], mine, "x2", j, ((x + k) % 4, sq, tn))
        local(dd.at[j], mine, "x2", j)

    def b1(j):
        part = lax.dot_general(
            gv[...].reshape(1024, HB), wj(j), (((1,), (1,)), ((), ())), preferred_element_type=F32
        )
        p[j] = part.astype(BF).reshape(2, 4, 128, HB)
        put(p.at[j, 0, yo], q1.at[j, 0], "b1l", j, right)
        put(p.at[j, 1, yo], q1.at[j, 1], "b1r", j, left)

    def b2(j):
        wait(R("b1l", j), 128)
        p[j, 0, yr] = (p[j, 0, yr].astype(F32) + q1[j, 0].astype(F32)).astype(BF)
        put(p.at[j, :, yr], q2.at[j, 0], "b2", j, right)
        wait(R("b1r", j), 128)
        p[j, 1, yl] = (p[j, 1, yl].astype(F32) + q1[j, 1].astype(F32)).astype(BF)
        put(p.at[j, :, yl], q2.at[j, 1], "b2", j, left)

    def b3a(j):
        wait(R("b2", j), 512)
        total = p[j, :, y].astype(F32) + q2[j, 0].astype(F32) + q2[j, 1].astype(F32)
        s[j] = total.astype(BF).reshape(2, 8, 16, HB)
        for i, (lo, hi) in enumerate(near_sites(1 - zl)):
            put(s.at[j, lo, pl.ds(hi * 2, 2)], zz.at[j, i], "b3a", j, beside)

    def b3(j):
        wait(R("b3a", j), 128)
        for i, (lo, hi) in enumerate(near_sites(zl)):
            pair = s[j, lo, pl.ds(hi * 2, 2)].astype(F32) + zz[j, i].astype(F32)
            s2[j, i] = pair.astype(BF)
        for i, (lo, hi) in enumerate(near_sites(zl)):
            for c in range(2):
                cc = (co + c) % 2
                if i == 3 and c == 0:
                    local(s2.at[j, i, cc], z.at[j, tn], "b3", j)
                else:
                    put(s2.at[j, i, cc], z.at[j, tn], "b3", j, (x, lo * 4 + y, hi * 2 + cc))

    def b4(j):
        wait(R("b3", j), 128)
        mixed = jnp.dot(z[j].reshape(128, HB), tab[...], preferred_element_type=F32)
        rotate_to(mixed, t2, j)
        mine = ghid.at[r16(tn), cols(j)]
        for k in range(1, 8):
            to = (tn + k) % 8
            put(t2.at[j, to], mine, "b4", j, (x, sq, to))
        local(t2.at[j, tn], mine, "b4", j)

    def o1():
        op[...] = oa[...].astype(BF).reshape(4, 2, 128, HB)
        for k in range(4):
            put(op.at[k, 1 - co], oh.at[k], "o1", 0, twin)

    def o2s():
        wait(R("o1", 0), 512)
        for k in range(4):
            o2[k] = (op[k, co].astype(F32) + oh[k].astype(F32)).astype(BF)
        for k in range(1, 4):
            to = (zh + k) % 4
            put(o2.at[to], orx.at[k - 1], "o2", 0, (x, sq, to * 2 + co))

    def at(cond, *steps):
        @pl.when(cond)
        def _():
            for step in steps:
                step()

    g2()
    wcopy.wait()
    wait(R("g2", 0), 512)
    b1(0)
    b1(1)
    f2(0)
    f1(1)
    b2(0)
    b1(2)
    f2b(0)
    f2(1)
    f1(2)
    f3(0)

    @pl.loop(0, NB)
    def _(j):
        more = j + 1 < NB
        at(more, lambda: b2(j + 1))
        at(j + 3 < NB, lambda: f1(j + 3))
        b3a(j)
        at(j + 2 < NB, lambda: f2(j + 2))
        f4(j)
        b3(j)
        at(j + 3 < NB, lambda: b1(j + 3))
        at(more, lambda: f2b(j + 1), lambda: f3(j + 1))
        at(j >= 1, lambda: x2(j - 1))
        f5a(j)
        at(j + 1 == NB, o1)
        f5b(j)
        at(j + 1 == NB, o2s)
        b4(j)

    x2(NB - 1)

    wait(R("o2", 0), 384)
    total = o2[zh].astype(F32)
    for k in range(3):
        total = total + orx[k].astype(F32)
    out[...] = total.astype(BF)

    for name, n in (("g1", 384), ("g2", 512), ("o1", 512), ("o2", 384)):
        wait(S(name, 0), n)

    @pl.loop(0, NB)
    def _(j):
        wait(R("x2", j), 512)
        wait(R("b4", j), 128)
        for name, n in (("f1", 112), ("f2", 112), ("f2b", 128), ("f3l", 256), ("f3r", 256), ("f4", 256), ("x1", 384),
                        ("x2", 384), ("b1l", 128), ("b1r", 128), ("b2", 512), ("b3a", 128), ("b3", 112), ("b4", 112)):
            wait(S(name, j), n)


def body(hidden, weight, out_grad):
    vm = pltpu.VMEM
    ns = len(STAGES)
    return pl.pallas_call(
        kernel,
        name="rotated_projection",
        out_shape=(
            pltpu.VMEM((128, HB), BF),
            pltpu.VMEM((128, NB * HB), BF),
            pltpu.VMEM((NB * HB, HB), BF),
        ),
        in_specs=[pl.BlockSpec(memory_space=pl.ANY)] * 3,
        out_specs=(pl.BlockSpec(memory_space=pltpu.VMEM),) * 3,
        scratch_shapes=[
            vm((NB, 8, 16, HB), BF),
            vm((NB, 8, 16, HB), BF),
            vm((NB, 2, 4, 8, 16, HB), BF),
            vm((NB, 2, 4, 128, HB), BF),
            vm((NB, 2, 128, HB), BF),
            vm((NB, 2, 2, 128, HB), BF),
            vm((NB, 2, 8, 16, HB), BF),
            vm((NB, 4, 2, 16, HB), BF),
            vm((NB, 4, 2, 16, HB), BF),
            vm((NB, 8, 16, HB), BF),
            vm((NB, 8, 16, HB), BF),
            vm((NB, 4, 128, HB), BF),
            vm((NB, 3, 128, HB), BF),
            vm((NB, 128, HB), BF),
            vm((8, 128, HB), BF),
            vm((NB * HB, HB), BF),
            vm((1024, HB), F32),
            vm((4, 2, 128, HB), BF),
            vm((4, 128, HB), BF),
            vm((4, 128, HB), BF),
            vm((3, 128, HB), BF),
            vm((HB, HB), BF),
            pltpu.SemaphoreType.DMA((ns, NB)),
            pltpu.SemaphoreType.DMA((ns, NB)),
            pltpu.SemaphoreType.DMA,
        ],
        compiler_params=pltpu.CompilerParams(
            collective_id=0, has_side_effects=True, vmem_limit_bytes=54 * 1024 * 1024
        ),
    )(hidden, weight, out_grad)


def solution(mesh):
    in_specs = (P(("dp", "seq"), "tensor"), P("tensor", "seq"), P(("dp", "tensor"), "seq"))
    out_specs = (P(("dp", "tensor"), "seq"), P(("dp", "seq"), "tensor"), P("tensor", "seq"))
    return jax.shard_map(body, mesh=mesh, in_specs=in_specs, out_specs=out_specs, check_vma=False)
```

```python
import jax
import jax.numpy as jnp
from jax import lax
from jax.experimental import pallas as pl
from jax.experimental.pallas import tpu as pltpu
from jax.sharding import PartitionSpec as P

HB = 512
NB = 7
BF = jnp.bfloat16
F32 = jnp.float32
MESH = pl.DeviceIdType.MESH
STAGES = (
    "f1", "g1", "g2", "f2", "f2b", "f3l", "f3r", "f4", "x1", "x2",
    "b1l", "b1r", "b2", "b3a", "b3", "b4", "o1", "o2",
)


def parity_table():
    row = lax.broadcasted_iota(jnp.int32, (HB, HB), 0)
    col = lax.broadcasted_iota(jnp.int32, (HB, HB), 1)
    both = row & col
    both = both ^ (both >> 8)
    both = both ^ (both >> 4)
    both = both ^ (both >> 2)
    both = both ^ (both >> 1)
    return jnp.where((both & 1) == 1, -1.0, 1.0).astype(BF)


def walsh8(parts):
    for bit in (1, 2, 4):
        parts = [
            parts[i] + parts[i ^ bit] if i & bit == 0 else parts[i ^ bit] - parts[i]
            for i in range(8)
        ]
    return parts


def kernel(hid, wgt, ogr, out, ghid, gwgt, a, r, hg, p, q1, q2, s, zz, s2, z, t2, d, xr, dd, gv, wv, oa, op, oh, o2, orx, tab, recv, send, wsem):
    x = lax.axis_index("dp")
    sq = lax.axis_index("seq")
    tn = lax.axis_index("tensor")
    zl = sq // 4
    y = sq % 4
    yr = (y + 1) % 4
    yl = (y + 3) % 4
    yo = (y + 2) % 4
    right = (x, zl * 4 + yr, tn)
    left = (x, zl * 4 + yl, tn)
    zh = tn // 2
    co = tn % 2
    beside = (x, (1 - zl) * 4 + y, tn)
    twin = (x, sq, zh * 2 + 1 - co)

    def near_sites(lo):
        e = (zh + 3 + 2 * lo) % 4
        return ((0, e), (1, e), (1 - lo, (zh + 2) % 4), (lo, zh))

    def near_lo(k):
        return (zl, 0, 1 - zl, 1)[k]

    def R(name, j):
        return recv.at[STAGES.index(name), j]

    def S(name, j):
        return send.at[STAGES.index(name), j]

    def rows(n):
        return wv.at[pl.ds(0, n)]

    def wait(sem, n):
        pltpu.make_async_copy(rows(n), rows(n), sem).wait()

    def put(src, dst, name, j, dev, sname=None):
        pltpu.make_async_remote_copy(
            src_ref=src, dst_ref=dst, send_sem=S(sname or name, j), recv_sem=R(name, j),
            device_id=dev, device_id_type=MESH,
        ).start()

    def local(src, dst, name, j):
        pltpu.make_async_copy(src, dst, R(name, j)).start()

    def cols(j):
        return pl.ds(pl.multiple_of(j * HB, HB), HB)

    def r16(i):
        return pl.ds(pl.multiple_of(i * 16, 16), 16)

    wcopy = pltpu.make_async_copy(wgt, wv, wsem)
    wcopy.start()

    bar = pltpu.get_barrier_semaphore()
    peers = [(x, sq, (tn + k) % 8) for k in range(1, 8)]
    peers += [(x, (sq + 4) % 8, (tn + k) % 8) for k in range(8)]
    peers += [right, left]
    peers += [((x + k) % 4, sq, tn) for k in range(1, 4)]
    for dev in peers:
        pl.semaphore_signal(bar, inc=1, device_id=dev, device_id_type=MESH)
    pl.semaphore_wait(bar, len(peers))

    def f1(j):
        for k in range(1, 8):
            to = (tn + k) % 8
            put(hid.at[r16(to), cols(j)], a.at[j, tn], "f1", j, (x, sq, to))
        local(hid.at[r16(tn), cols(j)], a.at[j, tn], "f1", j)

    def g1(k):
        put(ogr, gv.at[tn], "g1", 0, (x, sq, (tn + 2 * k) % 8))

    def g0():
        put(ogr, gv.at[tn], "g2", 0, twin)
        local(ogr, gv.at[tn], "g1", 0)

    def g2():
        wait(R("g1", 0), 512)
        for k in range(1, 4):
            part = (tn + 2 * k) % 8
            put(gv.at[part], gv.at[part], "g2", 0, twin)

    g0()
    for k in (1, 3, 2):
        g1(k)
    f1(0)
    tab[...] = parity_table()
    oa[...] = jnp.zeros_like(oa)

    def rotate_to(mixed, dst, j):
        parts = walsh8([mixed[i * 16:(i + 1) * 16] for i in range(8)])
        for i in range(8):
            dst[j, i] = (parts[i] * (1.0 / 64.0)).astype(BF)

    def f2(j):
        wait(R("f1", j), 128)
        mixed = jnp.dot(a[j].reshape(128, HB), tab[...], preferred_element_type=F32)
        rotate_to(mixed, r, j)
        land = hg.at[j, zl, y, tn]
        for k in range(4):
            for c in range(2):
                to = ((zh + k) % 4) * 2 + (co + c) % 2
                if k == 0 and c == 0:
                    local(r.at[j, tn], land, "f2", j)
                else:
                    put(r.at[j, to], land, "f2", j, (x, near_lo(k) * 4 + y, to))

    def f2b(j):
        wait(R("f2", j), 128)
        for lo, hi in near_sites(zl):
            part = hg.at[j, lo, y, pl.ds(hi * 2, 2)]
            put(part, part, "f2b", j, beside)

    def f3(j):
        wait(R("f2b", j), 128)
        put(hg.at[j, :, y], hg.at[j, :, y], "f3l", j, right)
        put(hg.at[j, :, y], hg.at[j, :, y], "f3r", j, left)

    def f4(j):
        wait(R("f3l", j), 256)
        put(hg.at[j, 0, yl], hg.at[j, 0, yl], "f4", j, right)
        wait(R("f3r", j), 256)
        put(hg.at[j, 1, yr], hg.at[j, 1, yr], "f4", j, left)

    def wj(j):
        return wv[pl.ds(pl.multiple_of(j * HB, HB), HB), :]

    def f5a(j):
        wait(R("f4", j), 256)
        oa[...] += jnp.dot(hg[j].reshape(1024, HB), wj(j), preferred_element_type=F32)

    def f5b(j):
        grad = lax.dot_general(
            hg[j].reshape(1024, HB), gv[...].reshape(1024, HB), (((0,), (0,)), ((), ())),
            preferred_element_type=F32,
        )
        d[j] = (grad * (1.0 / 64.0)).astype(BF).reshape(4, 128, HB)
        for k in range(1, 4):
            to = (x + k) % 4
            put(d.at[j, to], xr.at[j, k - 1], "x1", j, (to, sq, tn))

    def x2(j):
        wait(R("x1", j), 384)
        total = d[j, x].astype(F32)
        for k in range(3):
            total = total + xr[j, k].astype(F32)
        dd[j] = total.astype(BF)
        mine = gwgt.at[pl.ds(pl.multiple_of(j * HB + x * 128, 128), 128)]
        for k in range(1, 4):
            put(dd.at[j], mine, "x2", j, ((x + k) % 4, sq, tn))
        local(dd.at[j], mine, "x2", j)

    def b1(j):
        part = lax.dot_general(
            gv[...].reshape(1024, HB), wj(j), (((1,), (1,)), ((), ())), preferred_element_type=F32
        )
        p[j] = part.astype(BF).reshape(2, 4, 128, HB)
        put(p.at[j, 0, yo], q1.at[j, 0], "b1l", j, right)
        put(p.at[j, 1, yo], q1.at[j, 1], "b1r", j, left)

    def b2(j):
        wait(R("b1l", j), 128)
        p[j, 0, yr] = (p[j, 0, yr].astype(F32) + q1[j, 0].astype(F32)).astype(BF)
        put(p.at[j, :, yr], q2.at[j, 0], "b2", j, right)
        wait(R("b1r", j), 128)
        p[j, 1, yl] = (p[j, 1, yl].astype(F32) + q1[j, 1].astype(F32)).astype(BF)
        put(p.at[j, :, yl], q2.at[j, 1], "b2", j, left)

    def b3a(j):
        wait(R("b2", j), 512)
        total = p[j, :, y].astype(F32) + q2[j, 0].astype(F32) + q2[j, 1].astype(F32)
        s[j] = total.astype(BF).reshape(2, 8, 16, HB)
        for i, (lo, hi) in enumerate(near_sites(1 - zl)):
            put(s.at[j, lo, pl.ds(hi * 2, 2)], zz.at[j, i], "b3a", j, beside)

    def b3(j):
        wait(R("b3a", j), 128)
        for i, (lo, hi) in enumerate(near_sites(zl)):
            pair = s[j, lo, pl.ds(hi * 2, 2)].astype(F32) + zz[j, i].astype(F32)
            s2[j, i] = pair.astype(BF)
        for i, (lo, hi) in enumerate(near_sites(zl)):
            for c in range(2):
                cc = (co + c) % 2
                if i == 3 and c == 0:
                    local(s2.at[j, i, cc], z.at[j, tn], "b3", j)
                else:
                    put(s2.at[j, i, cc], z.at[j, tn], "b3", j, (x, lo * 4 + y, hi * 2 + cc))

    def b4(j):
        wait(R("b3", j), 128)
        mixed = jnp.dot(z[j].reshape(128, HB), tab[...], preferred_element_type=F32)
        rotate_to(mixed, t2, j)
        mine = ghid.at[r16(tn), cols(j)]
        for k in range(1, 8):
            to = (tn + k) % 8
            put(t2.at[j, to], mine, "b4", j, (x, sq, to))
        local(t2.at[j, tn], mine, "b4", j)

    def o1():
        op[...] = oa[...].astype(BF).reshape(4, 2, 128, HB)
        for k in (2, 1, 3, 0):
            q = (zh + k) % 4
            put(op.at[q, 1 - co], oh.at[q], "o1", q, twin)

    def o2s():
        for k in (2, 1, 3, 0):
            q = (zh + k) % 4
            wait(R("o1", q), 128)
            o2[q] = (op[q, co].astype(F32) + oh[q].astype(F32)).astype(BF)
            if k:
                put(o2.at[q], orx.at[k - 1], "o2", 0, (x, sq, q * 2 + co))

    def at(cond, *steps):
        @pl.when(cond)
        def _():
            for step in steps:
                step()

    g2()
    wcopy.wait()
    wait(R("g2", 0), 512)
    b1(0)
    b1(1)
    f2(0)
    f1(1)
    b2(0)
    b1(2)
    f2b(0)
    f2(1)
    f1(2)
    f3(0)

    @pl.loop(0, NB)
    def _(j):
        more = j + 1 < NB
        last = j + 1 == NB
        at(more, lambda: b2(j + 1))
        at(j + 3 < NB, lambda: f1(j + 3))
        at(j == 0, lambda: b3a(j))
        at(j + 2 < NB, lambda: f2(j + 2))
        at(last, lambda: b3(j))
        f4(j)
        at(more, lambda: b3(j))
        at(j + 3 < NB, lambda: b1(j + 3))
        at(more, lambda: f2b(j + 1), lambda: f3(j + 1), lambda: b3a(j + 1))
        at(jnp.logical_and(j >= 1, more), lambda: x2(j - 1))
        f5a(j)
        at(last, o1)
        f5b(j)
        at(last, lambda: x2(j - 1), o2s)
        b4(j)

    x2(NB - 1)

    wait(R("o2", 0), 384)
    total = o2[zh].astype(F32)
    for k in range(3):
        total = total + orx[k].astype(F32)
    out[...] = total.astype(BF)

    for name, n in (("g1", 384), ("g2", 512), ("o2", 384)):
        wait(S(name, 0), n)
    for k in range(4):
        wait(S("o1", k), 128)

    @pl.loop(0, NB)
    def _(j):
        wait(R("x2", j), 512)
        wait(R("b4", j), 128)
        for name, n in (("f1", 112), ("f2", 112), ("f2b", 128), ("f3l", 256), ("f3r", 256), ("f4", 256), ("x1", 384),
                        ("x2", 384), ("b1l", 128), ("b1r", 128), ("b2", 512), ("b3a", 128), ("b3", 112), ("b4", 112)):
            wait(S(name, j), n)


def body(hidden, weight, out_grad):
    vm = pltpu.VMEM
    ns = len(STAGES)
    return pl.pallas_call(
        kernel,
        name="rotated_projection",
        out_shape=(
            pltpu.VMEM((128, HB), BF),
            pltpu.VMEM((128, NB * HB), BF),
            pltpu.VMEM((NB * HB, HB), BF),
        ),
        in_specs=[pl.BlockSpec(memory_space=pl.ANY)] * 3,
        out_specs=(pl.BlockSpec(memory_space=pltpu.VMEM),) * 3,
        scratch_shapes=[
            vm((NB, 8, 16, HB), BF),
            vm((NB, 8, 16, HB), BF),
            vm((NB, 2, 4, 8, 16, HB), BF),
            vm((NB, 2, 4, 128, HB), BF),
            vm((NB, 2, 128, HB), BF),
            vm((NB, 2, 2, 128, HB), BF),
            vm((NB, 2, 8, 16, HB), BF),
            vm((NB, 4, 2, 16, HB), BF),
            vm((NB, 4, 2, 16, HB), BF),
            vm((NB, 8, 16, HB), BF),
            vm((NB, 8, 16, HB), BF),
            vm((NB, 4, 128, HB), BF),
            vm((NB, 3, 128, HB), BF),
            vm((NB, 128, HB), BF),
            vm((8, 128, HB), BF),
            vm((NB * HB, HB), BF),
            vm((1024, HB), F32),
            vm((4, 2, 128, HB), BF),
            vm((4, 128, HB), BF),
            vm((4, 128, HB), BF),
            vm((3, 128, HB), BF),
            vm((HB, HB), BF),
            pltpu.SemaphoreType.DMA((ns, NB)),
            pltpu.SemaphoreType.DMA((ns, NB)),
            pltpu.SemaphoreType.DMA,
        ],
        compiler_params=pltpu.CompilerParams(
            collective_id=0, has_side_effects=True, vmem_limit_bytes=54 * 1024 * 1024
        ),
    )(hidden, weight, out_grad)


def solution(mesh):
    in_specs = (P(("dp", "seq"), "tensor"), P("tensor", "seq"), P(("dp", "tensor"), "seq"))
    out_specs = (P(("dp", "tensor"), "seq"), P(("dp", "seq"), "tensor"), P("tensor", "seq"))
    return jax.shard_map(body, mesh=mesh, in_specs=in_specs, out_specs=out_specs, check_vma=False)
```

```python
import jax
import jax.numpy as jnp
from jax import lax
from jax.experimental import pallas as pl
from jax.experimental.pallas import tpu as pltpu
from jax.sharding import PartitionSpec as P

HB = 512
NB = 7
BF = jnp.bfloat16
F32 = jnp.float32
MESH = pl.DeviceIdType.MESH
STAGES = (
    "f1", "g1", "g2", "f2", "f2b", "f3l", "f3r", "f4", "x1", "x2",
    "b1l", "b1r", "b2", "b3a", "b3", "b4", "o1", "o2",
)


def parity_table():
    row = lax.broadcasted_iota(jnp.int32, (HB, HB), 0)
    col = lax.broadcasted_iota(jnp.int32, (HB, HB), 1)
    both = row & col
    both = both ^ (both >> 8)
    both = both ^ (both >> 4)
    both = both ^ (both >> 2)
    both = both ^ (both >> 1)
    return jnp.where((both & 1) == 1, -1.0, 1.0).astype(BF)


def walsh8(parts):
    for bit in (1, 2, 4):
        parts = [
            parts[i] + parts[i ^ bit] if i & bit == 0 else parts[i ^ bit] - parts[i]
            for i in range(8)
        ]
    return parts


def kernel(hid, wgt, ogr, out, ghid, gwgt, a, r, hg, p, q1, q2, s, zz, s2, z, t2, d, xr, dd, gv, wv, oa, op, oh, o2, orx, tab, recv, send, wsem):
    x = lax.axis_index("dp")
    sq = lax.axis_index("seq")
    tn = lax.axis_index("tensor")
    zl = sq // 4
    y = sq % 4
    yr = (y + 1) % 4
    yl = (y + 3) % 4
    yo = (y + 2) % 4
    right = (x, zl * 4 + yr, tn)
    left = (x, zl * 4 + yl, tn)
    zh = tn // 2
    co = tn % 2
    beside = (x, (1 - zl) * 4 + y, tn)
    twin = (x, sq, zh * 2 + 1 - co)

    def near_sites(lo):
        e = (zh + 3 + 2 * lo) % 4
        return ((0, e), (1, e), (1 - lo, (zh + 2) % 4), (lo, zh))

    def near_lo(k):
        return (zl, 0, 1 - zl, 1)[k]

    def R(name, j):
        return recv.at[STAGES.index(name), j]

    def S(name, j):
        return send.at[STAGES.index(name), j]

    def rows(n):
        return wv.at[pl.ds(0, n)]

    def wait(sem, n):
        pltpu.make_async_copy(rows(n), rows(n), sem).wait()

    def put(src, dst, name, j, dev, sname=None):
        pltpu.make_async_remote_copy(
            src_ref=src, dst_ref=dst, send_sem=S(sname or name, j), recv_sem=R(name, j),
            device_id=dev, device_id_type=MESH,
        ).start()

    def local(src, dst, name, j):
        pltpu.make_async_copy(src, dst, R(name, j)).start()

    def cols(j):
        return pl.ds(pl.multiple_of(j * HB, HB), HB)

    def r16(i):
        return pl.ds(pl.multiple_of(i * 16, 16), 16)

    wcopy = pltpu.make_async_copy(wgt, wv, wsem)
    wcopy.start()

    bar = pltpu.get_barrier_semaphore()
    peers = [(x, sq, (tn + k) % 8) for k in range(1, 8)]
    peers += [(x, (sq + 4) % 8, (tn + k) % 8) for k in range(8)]
    peers += [right, left]
    peers += [((x + k) % 4, sq, tn) for k in range(1, 4)]
    for dev in peers:
        pl.semaphore_signal(bar, inc=1, device_id=dev, device_id_type=MESH)
    pl.semaphore_wait(bar, len(peers))

    def f1(j):
        for k in range(1, 8):
            to = (tn + k) % 8
            put(hid.at[r16(to), cols(j)], a.at[j, tn], "f1", j, (x, sq, to))
        local(hid.at[r16(tn), cols(j)], a.at[j, tn], "f1", j)

    def g1(k):
        put(ogr, gv.at[tn], "g1", 0, (x, sq, (tn + 2 * k) % 8))

    def g0():
        put(ogr, gv.at[tn], "g2", 0, twin)
        local(ogr, gv.at[tn], "g1", 0)

    def g2():
        wait(R("g1", 0), 512)
        for k in range(1, 4):
            part = (tn + 2 * k) % 8
            put(gv.at[part], gv.at[part], "g2", 0, twin)

    g0()
    for k in (1, 3, 2):
        g1(k)
    f1(0)
    tab[...] = parity_table()
    oa[...] = jnp.zeros_like(oa)

    def rotate_to(mixed, dst, j):
        parts = walsh8([mixed[i * 16:(i + 1) * 16] for i in range(8)])
        for i in range(8):
            dst[j, i] = (parts[i] * (1.0 / 64.0)).astype(BF)

    def f2(j):
        wait(R("f1", j), 128)
        mixed = jnp.dot(a[j].reshape(128, HB), tab[...], preferred_element_type=F32)
        rotate_to(mixed, r, j)
        land = hg.at[j, zl, y, tn]
        for k in range(4):
            for c in range(2):
                to = ((zh + k) % 4) * 2 + (co + c) % 2
                if k == 0 and c == 0:
                    local(r.at[j, tn], land, "f2", j)
                else:
                    put(r.at[j, to], land, "f2", j, (x, near_lo(k) * 4 + y, to))

    def f2b(j):
        wait(R("f2", j), 128)
        for lo, hi in near_sites(zl):
            part = hg.at[j, lo, y, pl.ds(hi * 2, 2)]
            put(part, part, "f2b", j, beside)

    def f3(j):
        wait(R("f2b", j), 128)
        put(hg.at[j, :, y], hg.at[j, :, y], "f3l", j, right)
        put(hg.at[j, :, y], hg.at[j, :, y], "f3r", j, left)

    def f4(j):
        wait(R("f3l", j), 256)
        put(hg.at[j, 0, yl], hg.at[j, 0, yl], "f4", j, right)
        wait(R("f3r", j), 256)
        put(hg.at[j, 1, yr], hg.at[j, 1, yr], "f4", j, left)

    def wj(j):
        return wv[pl.ds(pl.multiple_of(j * HB, HB), HB), :]

    def f5a(j):
        wait(R("f4", j), 256)
        oa[...] += jnp.dot(hg[j].reshape(1024, HB), wj(j), preferred_element_type=F32)

    def f5b(j):
        grad = lax.dot_general(
            hg[j].reshape(1024, HB), gv[...].reshape(1024, HB), (((0,), (0,)), ((), ())),
            preferred_element_type=F32,
        )
        d[j] = (grad * (1.0 / 64.0)).astype(BF).reshape(4, 128, HB)
        for k in range(1, 4):
            to = (x + k) % 4
            put(d.at[j, to], xr.at[j, k - 1], "x1", j, (to, sq, tn))

    def x2(j):
        wait(R("x1", j), 384)
        total = d[j, x].astype(F32)
        for k in range(3):
            total = total + xr[j, k].astype(F32)
        dd[j] = total.astype(BF)
        mine = gwgt.at[pl.ds(pl.multiple_of(j * HB + x * 128, 128), 128)]
        for k in range(1, 4):
            put(dd.at[j], mine, "x2", j, ((x + k) % 4, sq, tn))
        local(dd.at[j], mine, "x2", j)

    def b1(j):
        part = lax.dot_general(
            gv[...].reshape(1024, HB), wj(j), (((1,), (1,)), ((), ())), preferred_element_type=F32
        )
        p[j] = part.astype(BF).reshape(2, 4, 128, HB)
        put(p.at[j, 0, yo], q1.at[j, 0], "b1l", j, right)
        put(p.at[j, 1, yo], q1.at[j, 1], "b1r", j, left)

    def b2(j):
        wait(R("b1l", j), 128)
        p[j, 0, yr] = (p[j, 0, yr].astype(F32) + q1[j, 0].astype(F32)).astype(BF)
        put(p.at[j, :, yr], q2.at[j, 0], "b2", j, right)
        wait(R("b1r", j), 128)
        p[j, 1, yl] = (p[j, 1, yl].astype(F32) + q1[j, 1].astype(F32)).astype(BF)
        put(p.at[j, :, yl], q2.at[j, 1], "b2", j, left)

    def b3a(j):
        wait(R("b2", j), 512)
        total = p[j, :, y].astype(F32) + q2[j, 0].astype(F32) + q2[j, 1].astype(F32)
        s[j] = total.astype(BF).reshape(2, 8, 16, HB)
        for i, (lo, hi) in enumerate(near_sites(1 - zl)):
            put(s.at[j, lo, pl.ds(hi * 2, 2)], zz.at[j, i], "b3a", j, beside)

    def b3(j):
        wait(R("b3a", j), 128)
        for i, (lo, hi) in enumerate(near_sites(zl)):
            pair = s[j, lo, pl.ds(hi * 2, 2)].astype(F32) + zz[j, i].astype(F32)
            s2[j, i] = pair.astype(BF)
        for i, (lo, hi) in enumerate(near_sites(zl)):
            for c in range(2):
                cc = (co + c) % 2
                if i == 3 and c == 0:
                    local(s2.at[j, i, cc], z.at[j, tn], "b3", j)
                else:
                    put(s2.at[j, i, cc], z.at[j, tn], "b3", j, (x, lo * 4 + y, hi * 2 + cc))

    def b4(j):
        wait(R("b3", j), 128)
        mixed = jnp.dot(z[j].reshape(128, HB), tab[...], preferred_element_type=F32)
        rotate_to(mixed, t2, j)
        mine = ghid.at[r16(tn), cols(j)]
        for k in range(1, 8):
            to = (tn + k) % 8
            put(t2.at[j, to], mine, "b4", j, (x, sq, to))
        local(t2.at[j, tn], mine, "b4", j)

    def o1():
        op[...] = oa[...].astype(BF).reshape(4, 2, 128, HB)
        for k in (2, 1, 3, 0):
            q = (zh + k) % 4
            put(op.at[q, 1 - co], oh.at[q], "o1", q, twin)

    def o2s():
        for k in (2, 1, 3, 0):
            q = (zh + k) % 4
            wait(R("o1", q), 128)
            o2[q] = (op[q, co].astype(F32) + oh[q].astype(F32)).astype(BF)
            if k:
                put(o2.at[q], orx.at[k - 1], "o2", 0, (x, sq, q * 2 + co))

    def at(cond, *steps):
        @pl.when(cond)
        def _():
            for step in steps:
                step()

    g2()
    wcopy.wait()
    wait(R("g2", 0), 512)
    b1(0)
    b1(1)
    f2(0)
    f1(1)
    b2(0)
    b1(2)
    f2b(0)
    f2(1)
    f1(2)
    f3(0)

    @pl.loop(0, NB)
    def _(j):
        more = j + 1 < NB
        last = j + 1 == NB
        at(more, lambda: b2(j + 1))
        at(jnp.logical_and(j >= 1, more), lambda: f2b(j + 1))
        at(j + 3 < NB, lambda: f1(j + 3))
        at(j == 0, lambda: b3a(j))
        at(j + 2 < NB, lambda: f2(j + 2))
        at(last, lambda: b3(j))
        f4(j)
        at(more, lambda: b3(j))
        at(j + 3 < NB, lambda: b1(j + 3))
        at(j == 0, lambda: f2b(j + 1))
        at(more, lambda: f3(j + 1), lambda: b3a(j + 1))
        at(jnp.logical_and(j >= 1, more), lambda: x2(j - 1))
        f5a(j)
        at(last, o1)
        f5b(j)
        at(last, lambda: x2(j - 1))
        b4(j)
        at(last, o2s)

    x2(NB - 1)

    wait(R("o2", 0), 384)
    total = o2[zh].astype(F32)
    for k in range(3):
        total = total + orx[k].astype(F32)
    out[...] = total.astype(BF)

    for name, n in (("g1", 384), ("g2", 512), ("o2", 384)):
        wait(S(name, 0), n)
    for k in range(4):
        wait(S("o1", k), 128)

    @pl.loop(0, NB)
    def _(j):
        wait(R("x2", j), 512)
        wait(R("b4", j), 128)
        for name, n in (("f1", 112), ("f2", 112), ("f2b", 128), ("f3l", 256), ("f3r", 256), ("f4", 256), ("x1", 384),
                        ("x2", 384), ("b1l", 128), ("b1r", 128), ("b2", 512), ("b3a", 128), ("b3", 112), ("b4", 112)):
            wait(S(name, j), n)


def body(hidden, weight, out_grad):
    vm = pltpu.VMEM
    ns = len(STAGES)
    return pl.pallas_call(
        kernel,
        name="rotated_projection",
        out_shape=(
            pltpu.VMEM((128, HB), BF),
            pltpu.VMEM((128, NB * HB), BF),
            pltpu.VMEM((NB * HB, HB), BF),
        ),
        in_specs=[pl.BlockSpec(memory_space=pl.ANY)] * 3,
        out_specs=(pl.BlockSpec(memory_space=pltpu.VMEM),) * 3,
        scratch_shapes=[
            vm((NB, 8, 16, HB), BF),
            vm((NB, 8, 16, HB), BF),
            vm((NB, 2, 4, 8, 16, HB), BF),
            vm((NB, 2, 4, 128, HB), BF),
            vm((NB, 2, 128, HB), BF),
            vm((NB, 2, 2, 128, HB), BF),
            vm((NB, 2, 8, 16, HB), BF),
            vm((NB, 4, 2, 16, HB), BF),
            vm((NB, 4, 2, 16, HB), BF),
            vm((NB, 8, 16, HB), BF),
            vm((NB, 8, 16, HB), BF),
            vm((NB, 4, 128, HB), BF),
            vm((NB, 3, 128, HB), BF),
            vm((NB, 128, HB), BF),
            vm((8, 128, HB), BF),
            vm((NB * HB, HB), BF),
            vm((1024, HB), F32),
            vm((4, 2, 128, HB), BF),
            vm((4, 128, HB), BF),
            vm((4, 128, HB), BF),
            vm((3, 128, HB), BF),
            vm((HB, HB), BF),
            pltpu.SemaphoreType.DMA((ns, NB)),
            pltpu.SemaphoreType.DMA((ns, NB)),
            pltpu.SemaphoreType.DMA,
        ],
        compiler_params=pltpu.CompilerParams(
            collective_id=0, has_side_effects=True, vmem_limit_bytes=54 * 1024 * 1024
        ),
    )(hidden, weight, out_grad)


def solution(mesh):
    in_specs = (P(("dp", "seq"), "tensor"), P("tensor", "seq"), P(("dp", "tensor"), "seq"))
    out_specs = (P(("dp", "tensor"), "seq"), P(("dp", "seq"), "tensor"), P("tensor", "seq"))
    return jax.shard_map(body, mesh=mesh, in_specs=in_specs, out_specs=out_specs, check_vma=False)
```
